32 devices in a mesh: contrast: 4 (over y, x), pa: 2 (over core), pb: 4 (over z).
Axes of the slice: x: 2, y: 2, z: 4, core: 2. Of those that a mesh axis runs over, the one named last changes fastest.
Arguments:
- image: float32 [4, 2, 128, 160, 128], P('contrast', None, 'pa', 'pb'), may hold values from -9 to 9
- coil_maps: bfloat16 [4, 2, 128, 160, 128], P(None, None, 'pa', 'pb'), may hold values from -2 to 2
- kspace: bfloat16 [4, 4, 2, 128, 160, 128], P('contrast', None, None, ('pa', 'pb')), may hold values from -4 to 4
- sampling: int32 [4, 128, 160, 128], P('contrast', ('pa', 'pb')), may hold values 0 or 1
- available: int32 [4], P('contrast'), may hold values from 0 to 1, as said below
Outputs:
- image_next: float32 [4, 2, 128, 160, 128], P('contrast', None, 'pa', 'pb')
- misfit: float32 [], replicated
The draws below stay inside these ranges and needn't reach their ends.
Inputs may be any that keep to these rules, and one draw needn't show every extreme that they name: `available`: at least one contrast is missing, and at most max(1, 1) are.
All inputs are finite; a program needn't handle non-finite values. No bound on the sum of `sampling` on one device may be relied on, other than what follows from the above.
Results may differ from the reference program's by a relative error of at most 0.0003.
Values sent between devices are 32-bit elements; how exact they have to be, the bound alone decides.
A program may use at most 128 MiB of HBM per device.

```python
import jax
import jax.numpy as jnp
from jax import lax

NX = 128
NY = 160
NZ = 128
COILS = 4
CON = 4


def draw_image(key, part):
    base_key = jax.random.fold_in(key, 0)
    extent = (CON, 2, NX, NY, NZ)
    strength = 0.5 + jnp.arange(CON, dtype=jnp.float32) / max(CON - 1, 1)
    strength = strength.reshape(CON, 1, 1, 1, 1)
    sample = jnp.clip(jax.random.normal(base_key, extent, jnp.float32), -4.0, 4.0)
    return sample * strength


def draw_kspace(key, part):
    extent = (CON, COILS, 2, NZ, NY, NX)
    envelope = 0.3 * (1.0 + 2.0 * jnp.arange(NZ, dtype=jnp.float32) / max(NZ - 1, 1))
    envelope = envelope.reshape(1, 1, 1, NZ, 1, 1)
    sample = jnp.clip(jax.random.normal(key, extent, jnp.float32), -4.0, 4.0)
    return (sample * envelope).astype(jnp.bfloat16)


def draw_available(key, part):
    order_key, count_key = jax.random.split(key)
    ordering = jax.random.permutation(order_key, CON)
    missing = jax.random.randint(count_key, (), 1, max(1, CON // 4) + 1)
    return (ordering >= missing).astype(jnp.int32)


def touch_ends(entries, key, least, high):
    longest = entries.shape.index(max(entries.shape))
    spots = []
    for shift in (0, 1):
        where = [jax.random.randint(jax.random.fold_in(key, axis), (), 0, length) for axis, length in enumerate(entries.shape)]
        where[longest] = (where[longest] + shift) % entries.shape[longest]
        spots.append(tuple(where))
    return entries.at[spots[0]].set(least).at[spots[1]].set(high)


def block_levels(stream_key, shape, cuts, smallest, top_value):
    def one(axis_at, parts):
        draws = jax.random.uniform(jax.random.fold_in(jax.random.fold_in(stream_key, 6), axis_at), (parts,), jnp.float32, smallest / len(cuts), top_value / len(cuts))
        return jnp.repeat(jnp.exp(draws), shape[axis_at] // parts).reshape((-1,) + (1,) * (len(shape) - axis_at - 1))

    factor_of = one(*cuts[0])
    for cut in cuts[1:]:
        factor_of = factor_of * one(*cut)
    return factor_of


def gaussian(key, dims, spread, limit, shards=(), kind=jnp.bfloat16):
    array = spread * jax.random.normal(key, dims, jnp.float32)
    if shards:
        array = array * block_levels(key, dims, shards, -0.22, 0.18)
    return jnp.clip(array, -limit, limit).astype(kind)


def setup_inputs(seed: int = 0) -> dict:
    seeds = jax.random.split(jax.random.key(seed), 6)
    image = draw_image(jax.random.fold_in(seeds[5], 71), 0)
    coil_maps = gaussian(seeds[1], (COILS, 2, NX, NY, NZ), (0.7 / COILS ** 0.5), 2.0, ((2, 2), (3, 4)))
    kspace = draw_kspace(jax.random.fold_in(seeds[5], 71), 0)
    sampling = touch_ends((jax.random.randint(seeds[3], (CON, NZ, NY, NX), 0, 3) < 1).astype(jnp.int32), jax.random.fold_in(seeds[3], 1), 0, 1)
    available = draw_available(jax.random.fold_in(seeds[5], 71), 0)
    return dict(image=image, coil_maps=coil_maps, kspace=kspace, sampling=sampling, available=available)


step_size = 1.0
threshold = 2.5

def reference(image, coil_maps, kspace, sampling, available):
    sensitivity = coil_maps[:, 0].astype(jnp.float32) + 1j * coil_maps[:, 1].astype(jnp.float32)

    def per_contrast(entry):
        pixels, measured, mask_rows, present_flag = entry
        weight_factor = mask_rows.astype(jnp.float32) * present_flag.astype(jnp.float32)
        complex_image = pixels[0] + 1j * pixels[1]

        def per_coil(running, coil_element):
            single_sensitivity, single_measurement = coil_element
            fourier_coefficients = jnp.transpose(jnp.fft.fftn(single_sensitivity * complex_image, norm='ortho'), (2, 1, 0))
            measurement_value = single_measurement[0].astype(jnp.float32) + 1j * single_measurement[1].astype(jnp.float32)
            kspace_residual = weight_factor * (fourier_coefficients - measurement_value)
            returned = jnp.fft.ifftn(jnp.transpose(kspace_residual, (2, 1, 0)), norm='ortho')
            combined = jnp.conj(single_sensitivity) * returned
            grad_re = running[0] + jnp.real(combined).astype(jnp.float32)
            grad_im = running[1] + jnp.imag(combined).astype(jnp.float32)
            res_re = jnp.real(kspace_residual)
            res_im = jnp.imag(kspace_residual)
            misfit = running[2] + jnp.sum(res_re * res_re + res_im * res_im).astype(jnp.float32)
            return ((grad_re, grad_im, misfit), None)
        initial = (jnp.zeros(pixels.shape[1:], jnp.float32), jnp.zeros(pixels.shape[1:], jnp.float32), jnp.zeros((), jnp.float32))
        totals, _ = lax.scan(per_coil, initial, (sensitivity, measured))
        return totals
    grad_re, grad_im, misfits = lax.map(per_contrast, (image, kspace, sampling, available))
    present = available.astype(jnp.float32)[:, None, None, None]
    moved_re = image[:, 0] - step_size * grad_re
    moved_im = image[:, 1] - step_size * grad_im
    energy = present * (moved_re * moved_re + moved_im * moved_im)
    norm_value = jnp.sqrt(lax.optimization_barrier(jnp.sum(energy, axis=0)))
    factor = jnp.maximum(norm_value - threshold, 0.0) / jnp.maximum(norm_value, threshold)
    shrink = present * factor[None]
    image_next = jnp.stack([moved_re * shrink, moved_im * shrink], axis=1)
    misfit = jnp.sum(misfits) / (2.0 * CON * COILS * NX * NY * NZ)
    return (image_next, misfit)
```

```python
import math

import jax
import jax.numpy as jnp
from jax import lax
from jax.sharding import PartitionSpec as P

step_size = 1.0
threshold = 2.5


def complex_table(length, sign_value):
    indices = lax.iota(jnp.int32, length)
    phases = indices[:, None] * indices[None, :] % length
    angles = phases.astype(jnp.float32) * (2.0 * math.pi / length)
    normalize = 1.0 / math.sqrt(length)
    real_part = jnp.cos(angles) * normalize
    imag_part = sign_value * jnp.sin(angles) * normalize
    upper_rows = jnp.stack([real_part, imag_part], axis=1)
    bottom = jnp.stack([-imag_part, real_part], axis=1)
    return jnp.stack([upper_rows, bottom], axis=0)


def contract(pattern, operand, table):
    return jnp.einsum(
        pattern, operand, table, precision=lax.Precision.HIGH, preferred_element_type=jnp.float32
    )


def per_device(image, coil_maps, kspace, sampling, available):
    groups_pa = lax.axis_size("pa")
    groups_pb = lax.axis_size("pb")
    pixels = image[0]
    x_rows = pixels.shape[1]
    y_rows = pixels.shape[2]
    depth_size = pixels.shape[3]
    width_x = x_rows * groups_pa
    width_y = y_rows * groups_pb
    plane_size = x_rows * y_rows
    coil_total = coil_maps.shape[0]
    depth_share = kspace.shape[3]
    present = available[0].astype(jnp.float32)
    weight_factor = sampling[0].astype(jnp.float32) * present
    forward_z = complex_table(depth_size, -1.0)
    forward_y = complex_table(width_y, -1.0).reshape(2, groups_pb, y_rows, 2, width_y)
    forward_x = complex_table(width_x, -1.0).reshape(2, groups_pa, x_rows, 2, width_x)
    inverse_z = complex_table(depth_size, 1.0)
    inverse_y = complex_table(width_y, 1.0).reshape(2, width_y, 2, groups_pb, y_rows)
    inverse_x = complex_table(width_x, 1.0).reshape(2, width_x, 2, groups_pa, x_rows)
    every_axis = ("contrast", "pa", "pb")
    members_total = lax.axis_size("contrast") * groups_pa * groups_pb

    def sensitivity(coil_index):
        return (
            coil_maps[coil_index, 0].astype(jnp.float32),
            coil_maps[coil_index, 1].astype(jnp.float32),
        )

    def prepare(coil_index):
        sens_re, sens_im = sensitivity(coil_index)
        prod_re = sens_re * pixels[0] - sens_im * pixels[1]
        prod_im = sens_re * pixels[1] + sens_im * pixels[0]
        spread = jnp.stack([prod_re, prod_im], axis=0).reshape(2, plane_size, depth_size)
        return contract("cmz,czdk->dkm", spread, forward_z)[None]

    def exchange_forward(transformed):
        return lax.all_to_all(transformed, ("pa", "pb"), split_axis=2, concat_axis=0, tiled=True)

    def exchange_back(sendable):
        return lax.all_to_all(sendable, ("pa", "pb"), split_axis=0, concat_axis=2, tiled=True)[0]

    def fourier(portion, coil_index):
        blocks = portion.reshape(groups_pa, groups_pb, 2, depth_share, x_rows, y_rows)
        partial_value = contract("aeczxy,ceyfl->afzxl", blocks, forward_y)
        fourier_coefficients = contract("afzxl,faxdk->dzlk", partial_value, forward_x)
        kspace_residual = weight_factor * (
            fourier_coefficients - kspace[0, coil_index].astype(jnp.float32)
        )
        misfit_part = jnp.sum(kspace_residual * kspace_residual)
        one_partial_value = contract("czlk,ckfax->afzlx", kspace_residual, inverse_x)
        spatial = contract("afzlx,fldey->aedzxy", one_partial_value, inverse_y)
        return (
            spatial.reshape(groups_pa * groups_pb, 2, depth_share, plane_size),
            misfit_part,
        )

    def recover(received, coil_index, first_row, rows):
        image_part = contract("ckm,ckdz->dmz", received, inverse_z)
        image_part = image_part.reshape(2, rows, y_rows, depth_size)
        sens_re, sens_im = sensitivity(coil_index)
        sens_re = sens_re[first_row : first_row + rows]
        sens_im = sens_im[first_row : first_row + rows]
        return (
            sens_re * image_part[0] + sens_im * image_part[1],
            sens_re * image_part[1] - sens_im * image_part[0],
        )

    cut = x_rows - x_rows // 4
    halves = ((0, cut), (cut, x_rows - cut))
    last = coil_total - 1
    arrivals = {}
    outgoing = {}
    returned = {}
    misfit_parts = {}
    sent = [prepare(coil_index) for coil_index in range(coil_total)]
    steps = exchange_order(coil_total)
    for kind, coil_index in steps:
        if kind == "forward":
            arrivals[coil_index] = exchange_forward(sent[coil_index])
        else:
            returned[coil_index] = exchange_back(outgoing[coil_index])
        if kind == "forward":
            outgoing[coil_index], misfit_parts[coil_index] = fourier(
                arrivals[coil_index], coil_index
            )
    misfit_local = sum(misfit_parts[coil_index] for coil_index in range(coil_total))
    scalar_block = jnp.full((members_total, 128), misfit_local, jnp.float32)
    gathered = lax.all_to_all(
        scalar_block, every_axis, split_axis=0, concat_axis=0, tiled=True
    )
    misfit_sum = jnp.sum(gathered[:, 0])
    final = []
    for first_row, rows in halves:
        piece = outgoing[last][..., first_row * y_rows : (first_row + rows) * y_rows]
        final.append(exchange_back(piece))
    total_re = pixels[0]
    total_im = pixels[1]
    for coil_index in range(last):
        one_re, one_im = recover(returned[coil_index], coil_index, 0, x_rows)
        total_re = total_re - step_size * one_re
        total_im = total_im - step_size * one_im
    total_re, total_im = lax.optimization_barrier((total_re, total_im))
    results = []
    for (first_row, rows), piece in zip(halves, final):
        one_re, one_im = recover(piece, last, first_row, rows)
        moved_re = total_re[first_row : first_row + rows] - step_size * one_re
        moved_im = total_im[first_row : first_row + rows] - step_size * one_im
        energy = present * (moved_re * moved_re + moved_im * moved_im)
        moved_re, moved_im, energy = lax.optimization_barrier((moved_re, moved_im, energy))
        energy_total = sum_contrasts(energy)
        norm_value = jnp.sqrt(energy_total)
        factor = jnp.maximum(norm_value - threshold, 0.0) / jnp.maximum(norm_value, threshold)
        shrink = present * factor
        results.append(jnp.stack([moved_re * shrink, moved_im * shrink], axis=0))
    result = jnp.concatenate(results, axis=1)[None]
    count_all = (
        lax.axis_size("contrast") * image.shape[0] * coil_total * width_x * width_y * depth_size
    )
    return (result, misfit_sum / (2.0 * count_all))


def exchange_order(coil_total):
    steps = [("forward", coil_index) for coil_index in range(min(2, coil_total))]
    for coil_index in range(coil_total):
        if coil_index + 2 < coil_total:
            steps.append(("forward", coil_index + 2))
        if coil_index < coil_total - 1:
            steps.append(("back", coil_index))
    return steps


def sum_contrasts(energy):
    size = lax.axis_size("contrast")
    if size & (size - 1):
        return lax.psum(energy, "contrast")
    strides = [1 << bit for bit in range(size.bit_length() - 1)]
    middle = energy.shape[0] // 2
    pieces = []
    for part, order in ((energy[:middle], strides), (energy[middle:], strides[::-1])):
        for stride in order:
            pairs = [(index, index ^ stride) for index in range(size)]
            part = part + lax.ppermute(part, "contrast", pairs)
        pieces.append(part)
    return jnp.concatenate(pieces, axis=0)


def solution(mesh):
    return jax.shard_map(
        per_device,
        mesh=mesh,
        in_specs=(
            P("contrast", None, "pa", "pb", None),
            P(None, None, "pa", "pb", None),
            P("contrast", None, None, ("pa", "pb"), None, None),
            P("contrast", ("pa", "pb"), None, None),
            P("contrast"),
        ),
        out_specs=(P("contrast", None, "pa", "pb", None), P()),
        check_vma=False,
    )
```

```python
import math

import jax
import jax.numpy as jnp
from jax import lax
from jax.sharding import PartitionSpec as P

step_size = 1.0
threshold = 2.5


def complex_table(length, sign_value):
    indices = lax.iota(jnp.int32, length)
    phases = indices[:, None] * indices[None, :] % length
    angles = phases.astype(jnp.float32) * (2.0 * math.pi / length)
    normalize = 1.0 / math.sqrt(length)
    real_part = jnp.cos(angles) * normalize
    imag_part = sign_value * jnp.sin(angles) * normalize
    upper_rows = jnp.stack([real_part, imag_part], axis=1)
    bottom = jnp.stack([-imag_part, real_part], axis=1)
    return jnp.stack([upper_rows, bottom], axis=0)


def contract(pattern, operand, table):
    return jnp.einsum(
        pattern, operand, table, precision=lax.Precision.HIGH, preferred_element_type=jnp.float32
    )


def per_device(image, coil_maps, kspace, sampling, available):
    groups_pa = lax.axis_size("pa")
    groups_pb = lax.axis_size("pb")
    pixels = image[0]
    x_rows = pixels.shape[1]
    y_rows = pixels.shape[2]
    depth_size = pixels.shape[3]
    width_x = x_rows * groups_pa
    width_y = y_rows * groups_pb
    plane_size = x_rows * y_rows
    coil_total = coil_maps.shape[0]
    depth_share = kspace.shape[3]
    present = available[0].astype(jnp.float32)
    weight_factor = sampling[0].astype(jnp.float32) * present
    forward_z = complex_table(depth_size, -1.0)
    forward_y = complex_table(width_y, -1.0).reshape(2, groups_pb, y_rows, 2, width_y)
    forward_x = complex_table(width_x, -1.0).reshape(2, groups_pa, x_rows, 2, width_x)
    inverse_z = complex_table(depth_size, 1.0)
    inverse_y = complex_table(width_y, 1.0).reshape(2, width_y, 2, groups_pb, y_rows)
    inverse_x = complex_table(width_x, 1.0).reshape(2, width_x, 2, groups_pa, x_rows)
    every_axis = ("contrast", "pa", "pb")
    members_total = lax.axis_size("contrast") * groups_pa * groups_pb

    cut = x_rows - x_rows // 4
    halves = ((0, cut), (cut, x_rows - cut))

    def sensitivity(coil_index):
        return (
            coil_maps[coil_index, 0].astype(jnp.float32),
            coil_maps[coil_index, 1].astype(jnp.float32),
        )

    def prepare(coil_index):
        sens_re, sens_im = sensitivity(coil_index)
        prod_re = sens_re * pixels[0] - sens_im * pixels[1]
        prod_im = sens_re * pixels[1] + sens_im * pixels[0]
        spread = jnp.stack([prod_re, prod_im], axis=0).reshape(2, plane_size, depth_size)
        return contract("cmz,czdk->dkm", spread, forward_z)[None]

    def exchange_forward(transformed):
        return lax.all_to_all(transformed, ("pa", "pb"), split_axis=2, concat_axis=0, tiled=True)

    def exchange_back(sendable):
        return lax.all_to_all(sendable, ("pa", "pb"), split_axis=0, concat_axis=sendable.ndim - 2, tiled=True)[0]

    def fourier(portion, coil_index):
        blocks = portion.reshape(groups_pa, groups_pb, 2, depth_share, x_rows, y_rows)
        partial_value = contract("aeczxy,ceyfl->afzxl", blocks, forward_y)
        fourier_coefficients = contract("afzxl,faxdk->dzlk", partial_value, forward_x)
        kspace_residual = weight_factor * (
            fourier_coefficients - kspace[0, coil_index].astype(jnp.float32)
        )
        misfit_part = jnp.sum(kspace_residual * kspace_residual)
        one_partial_value = contract("czlk,ckfax->afzlx", kspace_residual, inverse_x)
        spatial = contract("afzlx,fldey->aedzxy", one_partial_value, inverse_y)
        pieces = [
            spatial[..., first_row : first_row + rows, :].reshape(
                groups_pa * groups_pb, 2, depth_share, rows * y_rows
            )
            for first_row, rows in halves
        ]
        return pieces, misfit_part

    def recover(received, coil_index, first_row, rows):
        image_part = contract("ckm,ckdz->dmz", received, inverse_z)
        image_part = image_part.reshape(2, rows, y_rows, depth_size)
        sens_re, sens_im = sensitivity(coil_index)
        sens_re = sens_re[first_row : first_row + rows]
        sens_im = sens_im[first_row : first_row + rows]
        return (
            sens_re * image_part[0] + sens_im * image_part[1],
            sens_re * image_part[1] - sens_im * image_part[0],
        )

    arrivals = {}
    outgoing = {}
    returned = {}
    misfit_parts = {}
    sent = [prepare(coil_index) for coil_index in range(coil_total)]
    steps = exchange_order(coil_total)
    for kind, coil_index in steps:
        if kind == "forward":
            arrivals[coil_index] = exchange_forward(sent[coil_index])
        else:
            returned[coil_index] = exchange_back(outgoing[coil_index][0])
        if kind == "forward":
            outgoing[coil_index], misfit_parts[coil_index] = fourier(
                arrivals[coil_index], coil_index
            )
    misfit_local = sum(misfit_parts[coil_index] for coil_index in range(coil_total))
    scalar_block = jnp.full((members_total, 128), misfit_local, jnp.float32)
    gathered = lax.all_to_all(
        scalar_block, every_axis, split_axis=0, concat_axis=0, tiled=True
    )
    misfit_sum = jnp.sum(gathered[:, 0])
    bundle = jnp.stack([outgoing[coil_index][1] for coil_index in range(coil_total)], axis=1)
    remainder = exchange_back(bundle)
    received = (returned, remainder)
    results = []
    for part_index, (first_row, rows) in enumerate(halves):
        moved_re = pixels[0, first_row : first_row + rows]
        moved_im = pixels[1, first_row : first_row + rows]
        for coil_index in range(coil_total):
            one_re, one_im = recover(received[part_index][coil_index], coil_index, first_row, rows)
            moved_re = moved_re - step_size * one_re
            moved_im = moved_im - step_size * one_im
        energy = present * (moved_re * moved_re + moved_im * moved_im)
        energy_total = sum_contrasts(energy)
        norm_value = jnp.sqrt(energy_total)
        factor = jnp.maximum(norm_value - threshold, 0.0) / jnp.maximum(norm_value, threshold)
        shrink = present * factor
        results.append(jnp.stack([moved_re * shrink, moved_im * shrink], axis=0))
    result = jnp.concatenate(results, axis=1)[None]
    count_all = (
        lax.axis_size("contrast") * image.shape[0] * coil_total * width_x * width_y * depth_size
    )
    return (result, misfit_sum / (2.0 * count_all))


def exchange_order(coil_total):
    steps = [("forward", coil_index) for coil_index in range(min(2, coil_total))]
    for coil_index in range(coil_total):
        if coil_index + 2 < coil_total:
            steps.append(("forward", coil_index + 2))
        steps.append(("back", coil_index))
    return steps


def sum_contrasts(energy):
    size = lax.axis_size("contrast")
    if size & (size - 1):
        return lax.psum(energy, "contrast")
    strides = [1 << bit for bit in range(size.bit_length() - 1)]
    middle = energy.shape[0] // 2
    pieces = []
    for part, order in ((energy[:middle], strides), (energy[middle:], strides[::-1])):
        for stride in order:
            pairs = [(index, index ^ stride) for index in range(size)]
            part = part + lax.ppermute(part, "contrast", pairs)
        pieces.append(part)
    return jnp.concatenate(pieces, axis=0)


def solution(mesh):
    return jax.shard_map(
        per_device,
        mesh=mesh,
        in_specs=(
            P("contrast", None, "pa", "pb", None),
            P(None, None, "pa", "pb", None),
            P("contrast", None, None, ("pa", "pb"), None, None),
            P("contrast", ("pa", "pb"), None, None),
            P("contrast"),
        ),
        out_specs=(P("contrast", None, "pa", "pb", None), P()),
        check_vma=False,
    )
```

```python
import math

import jax
import jax.numpy as jnp
from jax import lax
from jax.sharding import PartitionSpec as P

step_size = 1.0
threshold = 2.5


def complex_table(length, sign_value):
    indices = lax.iota(jnp.int32, length)
    phases = indices[:, None] * indices[None, :] % length
    angles = phases.astype(jnp.float32) * (2.0 * math.pi / length)
    normalize = 1.0 / math.sqrt(length)
    real_part = jnp.cos(angles) * normalize
    imag_part = sign_value * jnp.sin(angles) * normalize
    upper_rows = jnp.stack([real_part, imag_part], axis=1)
    bottom = jnp.stack([-imag_part, real_part], axis=1)
    return jnp.stack([upper_rows, bottom], axis=0)


def contract(pattern, operand, table):
    return jnp.einsum(
        pattern, operand, table, precision=lax.Precision.HIGH, preferred_element_type=jnp.float32
    )


def per_device(image, coil_maps, kspace, sampling, available):
    groups_pa = lax.axis_size("pa")
    groups_pb = lax.axis_size("pb")
    pixels = image[0]
    x_rows = pixels.shape[1]
    y_rows = pixels.shape[2]
    depth_size = pixels.shape[3]
    width_x = x_rows * groups_pa
    width_y = y_rows * groups_pb
    plane_size = x_rows * y_rows
    coil_total = coil_maps.shape[0]
    depth_share = kspace.shape[3]
    present = available[0].astype(jnp.float32)
    weight_factor = sampling[0].astype(jnp.float32) * present
    forward_z = complex_table(depth_size, -1.0)
    forward_y = complex_table(width_y, -1.0).reshape(2, groups_pb, y_rows, 2, width_y)
    forward_x = complex_table(width_x, -1.0).reshape(2, groups_pa, x_rows, 2, width_x)
    inverse_z = complex_table(depth_size, 1.0)
    inverse_y = complex_table(width_y, 1.0).reshape(2, width_y, 2, groups_pb, y_rows)
    inverse_x = complex_table(width_x, 1.0).reshape(2, width_x, 2, groups_pa, x_rows)
    every_axis = ("contrast", "pa", "pb")
    members_total = lax.axis_size("contrast") * groups_pa * groups_pb

    def sensitivity(coil_index):
        return (
            coil_maps[coil_index, 0].astype(jnp.float32),
            coil_maps[coil_index, 1].astype(jnp.float32),
        )

    def prepare(coil_index):
        sens_re, sens_im = sensitivity(coil_index)
        prod_re = sens_re * pixels[0] - sens_im * pixels[1]
        prod_im = sens_re * pixels[1] + sens_im * pixels[0]
        spread = jnp.stack([prod_re, prod_im], axis=0).reshape(2, plane_size, depth_size)
        return contract("cmz,czdk->dkm", spread, forward_z)[None]

    def exchange_forward(transformed):
        return lax.all_to_all(transformed, ("pa", "pb"), split_axis=2, concat_axis=0, tiled=True)

    def exchange_back(sendable):
        return lax.all_to_all(sendable, ("pa", "pb"), split_axis=0, concat_axis=2, tiled=True)[0]

    def fourier(portion, coil_index):
        blocks = portion.reshape(groups_pa, groups_pb, 2, depth_share, x_rows, y_rows)
        partial_value = contract("aeczxy,ceyfl->afzxl", blocks, forward_y)
        fourier_coefficients = contract("afzxl,faxdk->dzlk", partial_value, forward_x)
        kspace_residual = weight_factor * (
            fourier_coefficients - kspace[0, coil_index].astype(jnp.float32)
        )
        misfit_part = jnp.sum(kspace_residual * kspace_residual)
        one_partial_value = contract("czlk,ckfax->afzlx", kspace_residual, inverse_x)
        spatial = contract("afzlx,fldey->aedzxy", one_partial_value, inverse_y)
        packed = spatial.reshape(groups_pa * groups_pb, 2, depth_share, plane_size)
        return packed, misfit_part

    def recover(received, coil_index, first_row, rows):
        image_part = contract("ckm,ckdz->dmz", received, inverse_z)
        image_part = image_part.reshape(2, rows, y_rows, depth_size)
        sens_re, sens_im = sensitivity(coil_index)
        sens_re = sens_re[first_row : first_row + rows]
        sens_im = sens_im[first_row : first_row + rows]
        return (
            sens_re * image_part[0] + sens_im * image_part[1],
            sens_re * image_part[1] - sens_im * image_part[0],
        )

    cut = x_rows - x_rows * 3 // 8
    halves = ((0, cut), (cut, x_rows - cut))
    last = coil_total - 1
    arrivals = {}
    outgoing = {}
    returned = {}
    misfit_parts = {}
    sent = [prepare(coil_index) for coil_index in range(coil_total)]
    steps = exchange_order(coil_total)
    for kind, coil_index in steps:
        if kind == "forward":
            arrivals[coil_index] = exchange_forward(sent[coil_index])
        else:
            returned[coil_index] = exchange_back(outgoing[coil_index])
        if kind == "forward":
            outgoing[coil_index], misfit_parts[coil_index] = fourier(
                arrivals[coil_index], coil_index
            )
    misfit_local = sum(misfit_parts[coil_index] for coil_index in range(coil_total))
    scalar_block = jnp.full((members_total, 128), misfit_local, jnp.float32)
    gathered = lax.all_to_all(
        scalar_block, every_axis, split_axis=0, concat_axis=0, tiled=True
    )
    misfit_sum = jnp.sum(gathered[:, 0])
    final = []
    for first_row, rows in halves:
        piece = outgoing[last][..., first_row * y_rows : (first_row + rows) * y_rows]
        final.append(exchange_back(piece))
    total_re = pixels[0]
    total_im = pixels[1]
    for coil_index in range(last):
        one_re, one_im = recover(returned[coil_index], coil_index, 0, x_rows)
        total_re = total_re - step_size * one_re
        total_im = total_im - step_size * one_im
    total_re, total_im = lax.optimization_barrier((total_re, total_im))
    results = []
    for (first_row, rows), piece in zip(halves, final):
        one_re, one_im = recover(piece, last, first_row, rows)
        moved_re = total_re[first_row : first_row + rows] - step_size * one_re
        moved_im = total_im[first_row : first_row + rows] - step_size * one_im
        energy = present * (moved_re * moved_re + moved_im * moved_im)
        moved_re, moved_im, energy = lax.optimization_barrier((moved_re, moved_im, energy))
        energy_total = sum_contrasts(energy)
        norm_value = jnp.sqrt(energy_total)
        factor = jnp.maximum(norm_value - threshold, 0.0) / jnp.maximum(norm_value, threshold)
        shrink = present * factor
        results.append(jnp.stack([moved_re * shrink, moved_im * shrink], axis=0))
    result = jnp.concatenate(results, axis=1)[None]
    count_all = (
        lax.axis_size("contrast") * image.shape[0] * coil_total * width_x * width_y * depth_size
    )
    return (result, misfit_sum / (2.0 * count_all))


def exchange_order(coil_total):
    steps = [("forward", coil_index) for coil_index in range(min(2, coil_total))]
    for coil_index in range(coil_total):
        if coil_index + 2 < coil_total:
            steps.append(("forward", coil_index + 2))
        if coil_index < coil_total - 1:
            steps.append(("back", coil_index))
    return steps


def sum_contrasts(energy):
    size = lax.axis_size("contrast")
    if size & (size - 1):
        return lax.psum(energy, "contrast")
    strides = [1 << bit for bit in range(size.bit_length() - 1)]
    middle = energy.shape[0] // 2
    pieces = []
    for part, order in ((energy[:middle], strides), (energy[middle:], strides[::-1])):
        for stride in order:
            pairs = [(index, index ^ stride) for index in range(size)]
            part = part + lax.ppermute(part, "contrast", pairs)
        pieces.append(part)
    return jnp.concatenate(pieces, axis=0)


def solution(mesh):
    return jax.shard_map(
        per_device,
        mesh=mesh,
        in_specs=(
            P("contrast", None, "pa", "pb", None),
            P(None, None, "pa", "pb", None),
            P("contrast", None, None, ("pa", "pb"), None, None),
            P("contrast", ("pa", "pb"), None, None),
            P("contrast"),
        ),
        out_specs=(P("contrast", None, "pa", "pb", None), P()),
        check_vma=False,
    )
```
